128 devices in a mesh: req: 8 (over x, core), exp: 16 (over y, z).
Axes of the slice: x: 4, y: 4, z: 4, core: 2. Of those that a mesh axis runs over, the one named last changes fastest.
Arguments:
- tokens: bfloat16 [128, 64, 1536], P(('exp', 'req')), may hold values from -6 to 6
- parents: int32 [128, 64], P(('exp', 'req')), may hold values from -1 to 62, as said below
- accepted: int32 [128, 8], P(('exp', 'req')), may hold values from 0 to 63, as said below
- lengths: int32 [128], P('exp'), may hold values from 1 to 1024, as said below
- cache: bfloat16 [128, 1024, 1024], P('exp', None, 'req')
- attn_gain: float32 [1536], replicated, may hold values from 0.25 to 1.75
- qkv_weight: bfloat16 [1536, 2560], P(None, 'exp'), may hold values from -0.15625 to 0.15625
- out_weight: bfloat16 [1536, 1536], P('exp'), may hold values from -0.625 to 0.625
- moe_gain: float32 [1536], replicated, may hold values from 0.25 to 1.75
- router_weight: bfloat16 [1536, 16], replicated, may hold values from -0.3125 to 0.3125
- routes: int32 [128, 64, 2], P(('exp', 'req')), may hold values from 0 to 15, all different within a row; in each aligned block of 64 rows (0 to 63, 64 to 127, ..., all dimensions but the last counted through in order) at most 16 rows name the same one
- gate_up_weight: bfloat16 [16, 1536, 2048], P('exp'), may hold values from -0.15625 to 0.15625
- down_weight: bfloat16 [16, 1024, 1536], P('exp'), may hold values from -0.375 to 0.375
Outputs:
- layer_out: bfloat16 [128, 64, 1536], P(('exp', 'req'))
- appended: bfloat16 [128, 8, 1024], P(('exp', 'req'))
The draws below stay inside these ranges and needn't reach their ends.
Inputs may be any that keep to these rules, and one draw needn't show every extreme that they name: `parents`: draft token 0 has parent -1; every other token's parent is an earlier token. `accepted`: A path of the tree from token 0, in increasing order, each entry the parent of the next. `lengths`: some request has all 1024 positions. `routes`: within the rows of one device each expert is named by at most 16 rows, by exactly 16 in some.
All inputs are finite; a program needn't handle non-finite values.
Results may differ from the reference program's by a relative error of at most 0.014.
The reference program's roundings to bfloat16 on the way count: a program that leaves them out, or rounds other values in their place, can miss the bound.
Values may be sent and summed in bfloat16 or wider, within the bound.
A program may use at most 128 MiB of HBM per device.

```python
import math
import jax
import jax.numpy as jnp
import numpy as np
from jax import lax

D = 1536
HEADS = 24
KVH = 8
HD = 64
FF = 1024
TOP = 2
DRAFT = 64
ACCEPT = 8
REQ_DEV = 1
CTX = 1024
EXPERTS = 16
REQUESTS = 128
CAP = 16
N_REQ = 8
N_EXP = 16


def tree_helper(key):
    base = jax.random.fold_in(key, 11)
    top_ids = jnp.maximum(jnp.arange(DRAFT, dtype=jnp.int32), 1)
    parents = jax.random.randint(jax.random.fold_in(base, 1), (REQUESTS, DRAFT), 0, top_ids[None, :], dtype=jnp.int32)
    keys = jax.random.split(jax.random.fold_in(base, 2), REQUESTS)
    perms = jax.vmap(lambda single: jax.random.permutation(single, DRAFT - 1))(keys).astype(jnp.int32) + 1
    chosen = jnp.sort(perms[:, :ACCEPT - 1], axis=1)
    path = jnp.concatenate([jnp.zeros((REQUESTS, 1), jnp.int32), chosen], axis=1)
    rows = jnp.arange(REQUESTS, dtype=jnp.int32)[:, None]
    parents = parents.at[rows, path[:, 1:]].set(path[:, :-1])
    parents = parents.at[:, 0].set(-1)
    return (parents, path)


def draw_parents(key, part):
    parents, path = tree_helper(key)
    return parents


def draw_accepted(key, part):
    parents, path = tree_helper(key)
    return path


def draw_lengths(key, part):
    lens = jax.random.randint(jax.random.fold_in(key, 3), (REQUESTS,), 1, CTX + 1, dtype=jnp.int32)
    where_full = jax.random.randint(jax.random.fold_in(key, 4), (), 0, REQUESTS, dtype=jnp.int32)
    return lens.at[where_full].set(CTX)


def draw_cache(key, part):
    raw = jax.random.normal(jax.random.fold_in(key, 5), (REQUESTS, CTX, 2 * KVH * HD), jnp.float32)
    return raw.astype(jnp.bfloat16)


def level_of(rng, extent, cuts, smallest, high):
    def one(dim, parts):
        draws = jax.random.uniform(jax.random.fold_in(jax.random.fold_in(rng, 6), dim), (parts,), jnp.float32, smallest / len(cuts), high / len(cuts))
        return jnp.repeat(jnp.exp(draws), extent[dim] // parts).reshape((-1,) + (1,) * (len(extent) - dim - 1))

    factor_of = one(*cuts[0])
    for cut in cuts[1:]:
        factor_of = factor_of * one(*cut)
    return factor_of


def shared_out(key, own, number, rows, amount, top, bound, slope):
    sequence = jax.random.permutation(key, amount)
    packed, common = load_shares(amount, rows * top, bound, slope, True), load_shares(amount, rows * top, bound, slope, False)
    places = jnp.arange(amount)

    def named(sizes, offset_by):
        used = int((sizes > 0).sum())
        fixed = max(1, used // 4)
        passed = fixed + (places - fixed + offset_by * (used - fixed)) % max(1, amount - fixed)
        return jnp.zeros((amount,), jnp.int32).at[sequence[jnp.where(places < fixed, places, passed)]].set(jnp.asarray(sizes, jnp.int32))

    sizes = jnp.where(number % 4 == 0, named(packed, number // 4), named(common, number - number // 4 - 1))
    mixed = jax.random.permutation(jax.random.fold_in(own, 3), amount)
    source_of, receiver = mixed[0:amount // 2 * 2:2], mixed[1:amount // 2 * 2:2]
    margin = jnp.minimum(sizes[source_of] - 1, bound - sizes[receiver]) // 2
    margin = jnp.where((source_of == sequence[0]) | (receiver == sequence[0]) | (sizes[receiver] == 0), 0, jnp.maximum(margin, 0))
    passed = jax.random.randint(jax.random.fold_in(own, 4), (amount // 2,), 0, 1 << 20) % (margin + 1)
    sizes = sizes.at[source_of].add(-passed).at[receiver].add(passed)
    members = jnp.searchsorted(jnp.cumsum(sizes), jnp.arange(rows * top), side="right").astype(jnp.int32)
    listing = members.reshape(top, rows).T
    listing = listing[jax.random.permutation(jax.random.fold_in(own, 1), rows)]
    offset_by = jax.random.randint(jax.random.fold_in(own, 2), (rows, 1), 0, top)
    return jnp.take_along_axis(listing, (jnp.arange(top)[None, :] + offset_by) % top, axis=1)


def load_shares(amount, total, most, skew, full):
    portions = [(1 << 20) // math.isqrt(rank ** skew) + 1 for rank in range(1, amount + 1)]
    largest = most if full else min(most, max(-(-total // amount), total * portions[0] // sum(portions)))
    least = 1 if total - largest >= amount - 1 else 0
    given, spare = [largest] + [least] * (amount - 1), total - largest - least * (amount - 1)
    while spare > 0:
        free = [i for i in range(1, amount) if given[i] < largest] or [i for i in range(1, amount) if given[i] < most]
        mass, remaining = sum([portions[i] for i in free]), spare
        for i in free:
            more = min(most - given[i], max(1, remaining * portions[i] // mass), spare)
            given[i] = given[i] + more
            spare = spare - more
    return np.array(given)


def normal_values(rng, dims, spread, most, pieces=(), held_as=jnp.bfloat16):
    drawn = jax.random.normal(rng, dims, jnp.float32) * spread
    if len(pieces) > 0:
        drawn = level_of(rng, dims, pieces, -0.22, 0.18) * drawn
    return jnp.clip(drawn, min=-most, max=most).astype(held_as)


def setup_inputs(seed: int = 0) -> dict:
    key_list = jax.random.split(jax.random.key(seed), 14)
    tokens = normal_values(key_list[0], (REQUESTS, DRAFT, D), 1.0, 6.0, ((0, 128),))
    parents = draw_parents(jax.random.fold_in(key_list[13], 71), 0)
    accepted = draw_accepted(jax.random.fold_in(key_list[13], 71), 0)
    lengths = draw_lengths(jax.random.fold_in(key_list[13], 71), 0)
    cache = draw_cache(jax.random.fold_in(key_list[13], 71), 0)
    attn_gain = jnp.clip(1.0 + 0.15 * jax.random.normal(key_list[5], (D,), jnp.float32), 0.25, 1.75)
    qkv_weight = normal_values(key_list[6], (D, (HEADS + 2 * KVH) * HD), D ** -0.5, 0.15625, ((1, 16),))
    out_weight = normal_values(key_list[7], (HEADS * HD, D), (HEADS * HD // 16) ** -0.5, 0.625, ((0, 16),))
    moe_gain = jnp.clip(1.0 + 0.15 * jax.random.normal(key_list[8], (D,), jnp.float32), 0.25, 1.75)
    router_weight = normal_values(key_list[9], (D, EXPERTS), (D // 4) ** -0.5, 0.3125)
    routes_keys = jax.random.split(jax.random.fold_in(key_list[10], 1), REQUESTS * DRAFT // (REQ_DEV * DRAFT))
    routes_turns = jax.random.permutation(jax.random.fold_in(key_list[10], 3), REQUESTS * DRAFT // (REQ_DEV * DRAFT))
    routes = jax.vmap(lambda own, number: shared_out(jax.random.fold_in(key_list[10], 2), own, number, REQ_DEV * DRAFT, EXPERTS, TOP, CAP, 2))(routes_keys, routes_turns).reshape((REQUESTS, DRAFT, TOP))
    gate_up_weight = normal_values(key_list[11], (EXPERTS, D, 2 * FF), D ** -0.5, 0.15625, ((0, 16),))
    down_weight = normal_values(key_list[12], (EXPERTS, FF, D), (FF // 4) ** -0.5, 0.375, ((0, 16),))
    return dict(tokens=tokens, parents=parents, accepted=accepted, lengths=lengths, cache=cache, attn_gain=attn_gain, qkv_weight=qkv_weight, out_weight=out_weight, moe_gain=moe_gain, router_weight=router_weight, routes=routes, gate_up_weight=gate_up_weight, down_weight=down_weight)


NEG = -1e+30

def rms_norm(values, gain):
    wide = values.astype(jnp.float32)
    return wide * lax.rsqrt(lax.optimization_barrier(jnp.mean(wide * wide, axis=-1, keepdims=True)) + 1e-05) * gain

def ancestry(parents):
    size = parents.shape[-1]
    ids = jnp.arange(size, dtype=jnp.int32)
    reach = (parents[..., :, None] == ids).astype(jnp.float32) + jnp.eye(size, dtype=jnp.float32)
    for step in range(size.bit_length()):
        reach = jnp.minimum(jnp.einsum('...ij,...jk->...ik', reach, reach, precision=lax.Precision.HIGHEST), 1.0)
    return reach > 0.5

def attend(query, keys, values, live):
    scores = jnp.einsum('ikgd,tkd->ikgt', query.astype(jnp.float32), keys.astype(jnp.float32)) * HD ** (-0.5)
    mask = live[:, None, None, :]
    top = lax.optimization_barrier(jnp.max(jnp.where(mask, scores, NEG), axis=-1))
    weights = jnp.where(mask, jnp.exp(scores - top[..., None]), 0.0).astype(jnp.bfloat16)
    total = lax.optimization_barrier(jnp.sum(weights.astype(jnp.float32), axis=-1))
    acc = jnp.einsum('ikgt,tkd->ikgd', weights.astype(jnp.float32), values.astype(jnp.float32))
    count = query.shape[0]
    return (top.reshape(count, HEADS), total.reshape(count, HEADS), acc.reshape(count, HEADS, HD))

def finish(c_top, c_total, c_acc, d_top, d_total, d_acc):
    top = jnp.maximum(c_top, d_top)
    scale_c = jnp.exp(c_top - top)
    scale_d = jnp.exp(d_top - top)
    den = scale_c * c_total + scale_d * d_total
    num = c_acc * scale_c[..., None] + d_acc * scale_d[..., None]
    out = num / den[..., None]
    return out.reshape(out.shape[:-2] + (HEADS * HD,)).astype(jnp.bfloat16)

def reference(tokens, parents, accepted, lengths, cache, attn_gain, qkv_weight, out_weight, moe_gain, router_weight, routes, gate_up_weight, down_weight):
    group = HEADS // KVH
    qw = HEADS * HD
    kw = KVH * HD
    flat = tokens.reshape(REQUESTS * DRAFT, D)
    normed = rms_norm(flat, attn_gain).astype(jnp.bfloat16)
    qkv = jnp.dot(normed, qkv_weight, preferred_element_type=jnp.float32).astype(jnp.bfloat16)
    qkv = qkv.reshape(REQUESTS, DRAFT, qw + 2 * kw)
    tree = ancestry(parents)

    def attend_request(items):
        row, cache_row, length, tree_row = items
        query = row[:, :qw].reshape(DRAFT, KVH, group, HD)
        dkeys = row[:, qw:qw + kw].reshape(DRAFT, KVH, HD)
        dvals = row[:, qw + kw:].reshape(DRAFT, KVH, HD)
        d_top, d_total, d_acc = attend(query, dkeys, dvals, tree_row)
        pairs = cache_row.reshape(CTX, KVH, 2, HD)
        live = (jnp.arange(CTX, dtype=jnp.int32) < length)[None, :]
        c_top, c_total, c_acc = attend(query, pairs[:, :, 0], pairs[:, :, 1], live)
        return finish(c_top, c_total, c_acc, d_top, d_total, d_acc)
    attn = lax.map(attend_request, (qkv, cache, lengths, tree))
    attn = attn.reshape(REQUESTS * DRAFT, qw)
    resid = flat.astype(jnp.float32) + jnp.dot(attn, out_weight, preferred_element_type=jnp.float32)
    moe_in = rms_norm(resid, moe_gain).astype(jnp.bfloat16)
    logits = jnp.dot(moe_in, router_weight, preferred_element_type=jnp.float32)
    chosen = routes.reshape(REQUESTS * DRAFT, TOP).astype(jnp.int32)
    picked = jnp.take_along_axis(logits, chosen, axis=1)
    gate_first = jax.nn.sigmoid(picked[:, 0] - picked[:, 1])
    gate_second = jax.nn.sigmoid(picked[:, 1] - picked[:, 0])
    load = min(REQUESTS * DRAFT, N_REQ * N_EXP * CAP)

    def one_expert(total, expert):
        hit = jnp.any(chosen == expert, axis=1)
        order = jnp.argsort(1 - hit.astype(jnp.int32), stable=True)[:load].astype(jnp.int32)
        rows = moe_in[order]
        gate_up = lax.dynamic_index_in_dim(gate_up_weight, expert, 0, keepdims=False)
        down = lax.dynamic_index_in_dim(down_weight, expert, 0, keepdims=False)
        both = jnp.dot(rows, gate_up, preferred_element_type=jnp.float32)
        hidden = (jax.nn.silu(both[:, :FF]) * both[:, FF:]).astype(jnp.bfloat16)
        out = jnp.dot(hidden, down, preferred_element_type=jnp.float32).astype(jnp.bfloat16)
        weight = gate_first * (chosen[:, 0] == expert) + gate_second * (chosen[:, 1] == expert)
        weight = weight[order] * hit[order]
        return (total.at[order].add(out.astype(jnp.float32) * weight[:, None]), None)
    mixed, unused = lax.scan(one_expert, jnp.zeros((REQUESTS * DRAFT, D), jnp.float32), jnp.arange(EXPERTS, dtype=jnp.int32))
    layer_out = (resid + mixed).astype(jnp.bfloat16).reshape(REQUESTS, DRAFT, D)
    keys = qkv[:, :, qw:qw + kw].reshape(REQUESTS, DRAFT, KVH, 1, HD)
    vals = qkv[:, :, qw + kw:].reshape(REQUESTS, DRAFT, KVH, 1, HD)
    kv_pairs = jnp.concatenate([keys, vals], axis=3).reshape(REQUESTS, DRAFT, 2 * kw)
    appended = jnp.take_along_axis(kv_pairs, accepted.astype(jnp.int32)[:, :, None], axis=1)
    return (layer_out, appended)
```

```python
import jax
import jax.numpy as jnp
from jax import lax
from jax.sharding import PartitionSpec as P

HEADS = 24
KVH = 8
HD = 64
FF = 1024
TOP = 2


NEG = -1e30


def rms_norm(values, gain):
    wide = values.astype(jnp.float32)
    return wide * lax.rsqrt(jnp.mean(wide * wide, axis=-1, keepdims=True) + 1e-05) * gain


def pair_swap(values):
    n = lax.axis_size("req")
    return lax.ppermute(values, "req", [(i, i ^ 1) for i in range(n)])


def pair_join(core, mine, theirs, axis):
    first = jnp.concatenate([mine, theirs], axis=axis)
    second = jnp.concatenate([theirs, mine], axis=axis)
    return jnp.where(core == 0, first, second)


def ancestry(parents):
    size = parents.shape[-1]
    ids = jnp.arange(size, dtype=jnp.int32)
    reach = (parents[..., :, None] == ids).astype(jnp.float32) + jnp.eye(size, dtype=jnp.float32)
    for step in range(size.bit_length()):
        reach = jnp.minimum(
            jnp.einsum("...ij,...jk->...ik", reach, reach, precision=lax.Precision.HIGHEST), 1.0
        )
    return reach > 0.5


def attend(query, keys, values, live):
    scores = jnp.einsum("ikgd,tkd->ikgt", query, keys, preferred_element_type=jnp.float32) * HD ** (
        -0.5
    )
    mask = live[:, None, None, :]
    top = jnp.max(jnp.where(mask, scores, NEG), axis=-1)
    weights = jnp.where(mask, jnp.exp(scores - top[..., None]), 0.0).astype(jnp.bfloat16)
    total = jnp.sum(weights.astype(jnp.float32), axis=-1)
    acc = jnp.einsum("ikgt,tkd->ikgd", weights, values, preferred_element_type=jnp.float32)
    return (top, total, acc)


def finish(c_top, c_total, c_acc, d_top, d_total, d_acc):
    top = jnp.maximum(c_top, d_top)
    scale_c = jnp.exp(c_top - top)
    scale_d = jnp.exp(d_top - top)
    den = scale_c * c_total + scale_d * d_total
    num = c_acc * scale_c[..., None] + d_acc * scale_d[..., None]
    out = num / den[..., None]
    return out.reshape(out.shape[:-2] + (HEADS * HD,)).astype(jnp.bfloat16)


def on_device(
    tokens,
    parents,
    accepted,
    lengths,
    cache,
    attn_gain,
    qkv_weight,
    out_weight,
    moe_gain,
    router_weight,
    routes,
    gate_up_weight,
    down_weight,
):
    req_dev, draft, width = tokens.shape
    tok_rows = req_dev * draft
    group = HEADS // KVH
    q_width = HEADS * HD
    kv_width = KVH * HD
    span = cache.shape[1]
    group_req = cache.shape[0]
    n_req = lax.axis_size("req")
    flat = tokens.reshape(tok_rows, width)
    normed = rms_norm(flat, attn_gain).astype(jnp.bfloat16)
    core = lax.axis_index("req") % 2
    shard_cols = qkv_weight.shape[1]
    half_cols = shard_cols // 2
    qkv_half = lax.dynamic_slice_in_dim(qkv_weight, core * half_cols, half_cols, axis=1)
    qkv_half = lax.all_gather(qkv_half, "exp", axis=1, tiled=True)
    both_rows = jnp.concatenate([normed, pair_swap(normed)], axis=0)
    qkv_cols = jnp.dot(both_rows, qkv_half, preferred_element_type=jnp.float32).astype(
        jnp.bfloat16
    )
    n_shards = qkv_half.shape[1] // half_cols
    own_cols = qkv_cols[:tok_rows].reshape(tok_rows, n_shards, 1, half_cols)
    other_cols = pair_swap(qkv_cols[tok_rows:]).reshape(tok_rows, n_shards, 1, half_cols)
    qkv = pair_join(core, own_cols, other_cols, 2).reshape(tok_rows, n_shards * shard_cols)
    queries = qkv[:, :q_width].reshape(req_dev, draft, q_width)
    draft_keys = qkv[:, q_width : q_width + kv_width].reshape(req_dev, draft, KVH, HD)
    draft_values = qkv[:, q_width + kv_width :].reshape(req_dev, draft, KVH, HD)
    tree = ancestry(parents)

    def draft_request(items):
        query_row, key_row, value_row, tree_row = items
        return attend(query_row.reshape(draft, KVH, group, HD), key_row, value_row, tree_row)

    d_top, d_total, d_acc = jax.vmap(draft_request)((queries, draft_keys, draft_values, tree))
    d_top = d_top.reshape(req_dev, draft, HEADS)
    d_total = d_total.reshape(req_dev, draft, HEADS)
    d_acc = d_acc.reshape(req_dev, draft, HEADS, HD)
    kv_local = KVH // n_req
    q_local = HEADS // n_req
    live_all = jnp.arange(span, dtype=jnp.int32)[None, :] < lengths[:, None]
    local_pairs = cache.reshape(group_req, span, kv_local, 2, HD)
    split_queries = queries.reshape(req_dev, draft, n_req, q_local * HD)
    piece = lax.all_to_all(split_queries, "req", split_axis=2, concat_axis=0, tiled=True)
    count = piece.shape[1]
    query_all = piece.reshape(group_req, count, kv_local, group, HD)

    def cache_request(items):
        query_row, pair_row, live_row = items
        return attend(query_row, pair_row[:, :, 0], pair_row[:, :, 1], live_row[None, :])

    h_top, h_total, h_acc = jax.vmap(cache_request)((query_all, local_pairs, live_all))
    c_top = lax.all_to_all(
        h_top.astype(jnp.bfloat16), "req", split_axis=0, concat_axis=2, tiled=True
    ).astype(jnp.float32)
    c_total = lax.all_to_all(
        h_total.astype(jnp.bfloat16), "req", split_axis=0, concat_axis=2, tiled=True
    ).astype(jnp.float32)
    c_acc = lax.all_to_all(
        h_acc.reshape(group_req, count, 1, q_local * HD).astype(jnp.bfloat16),
        "req",
        split_axis=0,
        concat_axis=2,
        tiled=True,
    ).astype(jnp.float32)
    c_top = c_top.reshape(req_dev, draft, HEADS)
    c_total = c_total.reshape(req_dev, draft, HEADS)
    c_acc = c_acc.reshape(req_dev, draft, HEADS, HD)
    attn = finish(c_top, c_total, c_acc, d_top, d_total, d_acc).reshape(tok_rows, q_width)
    out_cols = out_weight.shape[1] // 2
    out_half = lax.dynamic_slice_in_dim(out_weight, core * out_cols, out_cols, axis=1)
    out_half = lax.all_gather(out_half, "exp", axis=0, tiled=True)
    attn_rows = jnp.concatenate([attn, pair_swap(attn)], axis=0)
    proj_cols = jnp.dot(attn_rows, out_half, preferred_element_type=jnp.float32)
    projected = pair_join(core, proj_cols[:tok_rows], pair_swap(proj_cols[tok_rows:]), 1)
    resid = flat.astype(jnp.float32) + projected
    moe_in = rms_norm(resid, moe_gain).astype(jnp.bfloat16)
    logits = jnp.dot(moe_in, router_weight, preferred_element_type=jnp.float32)
    experts = router_weight.shape[1]
    expert_ids = jnp.arange(experts, dtype=jnp.int32)
    chosen = routes.reshape(tok_rows, TOP)
    picked = jnp.sum(jnp.where(chosen[:, :, None] == expert_ids, logits[:, None, :], 0.0), axis=-1)
    gate_first = jax.nn.sigmoid(picked[:, 0] - picked[:, 1])
    gate_second = jax.nn.sigmoid(picked[:, 1] - picked[:, 0])
    capacity = max(2, 2 * tok_rows * TOP // experts)
    flat_ids = chosen.reshape(tok_rows * TOP)
    onehot = (flat_ids[:, None] == expert_ids).astype(jnp.int32)
    before = jnp.cumsum(onehot, axis=0) - onehot
    slot = jnp.sum(before * onehot, axis=1)
    position = (flat_ids * capacity + slot).reshape(tok_rows, TOP)
    select = position[:, :, None] == jnp.arange(experts * capacity, dtype=jnp.int32)
    placing = jnp.any(select, axis=1).astype(jnp.bfloat16)
    buffer = jnp.einsum("ts,td->sd", placing, moe_in, preferred_element_type=jnp.float32).astype(
        jnp.bfloat16
    )
    buffer = buffer.reshape(experts, capacity, width)
    received = lax.all_to_all(buffer, "exp", split_axis=0, concat_axis=0, tiled=True)
    count = received.shape[1]
    rows = received.reshape(experts * count, width)
    both = jnp.dot(rows, gate_up_weight[0], preferred_element_type=jnp.float32)
    hidden = (jax.nn.silu(both[:, :FF]) * both[:, FF:]).astype(jnp.bfloat16)
    result = jnp.dot(hidden, down_weight[0], preferred_element_type=jnp.float32).astype(
        jnp.bfloat16
    )
    back = lax.all_to_all(
        result.reshape(experts, count, width), "exp", split_axis=0, concat_axis=0, tiled=True
    )
    back_flat = back.reshape(experts * capacity, width)
    first = jnp.dot(
        select[:, 0].astype(jnp.bfloat16), back_flat, preferred_element_type=jnp.float32
    )
    second = jnp.dot(
        select[:, 1].astype(jnp.bfloat16), back_flat, preferred_element_type=jnp.float32
    )
    layer_out = (resid + gate_first[:, None] * first + gate_second[:, None] * second).astype(
        jnp.bfloat16
    )
    taking = (accepted[:, :, None] == jnp.arange(draft, dtype=jnp.int32)).astype(jnp.bfloat16)
    key_part = draft_keys.reshape(req_dev, draft, KVH, 1, HD)
    value_part = draft_values.reshape(req_dev, draft, KVH, 1, HD)
    kv_pairs = jnp.concatenate([key_part, value_part], axis=3).reshape(req_dev, draft, 2 * kv_width)
    appended = jnp.einsum(
        "rad,rdc->rac", taking, kv_pairs, preferred_element_type=jnp.float32
    ).astype(jnp.bfloat16)
    return (layer_out.reshape(req_dev, draft, width), appended)


def solution(mesh):
    placed = (
        P(("exp", "req"), None, None),
        P(("exp", "req"), None),
        P(("exp", "req"), None),
        P("exp"),
        P("exp", None, "req"),
        P(),
        P(None, "exp"),
        P("exp", None),
        P(),
        P(),
        P(("exp", "req"), None, None),
        P("exp", None, None),
        P("exp", None, None),
    )
    return jax.shard_map(
        on_device,
        mesh=mesh,
        in_specs=placed,
        out_specs=(P(("exp", "req"), None, None), P(("exp", "req"), None, None)),
        check_vma=False,
    )
```

```python
import jax
import jax.numpy as jnp
from jax import lax
from jax.sharding import PartitionSpec as P

HEADS = 24
KVH = 8
HD = 64
FF = 1024
TOP = 2


NEG = -1e30


def rms_norm(values, gain):
    wide = values.astype(jnp.float32)
    return wide * lax.rsqrt(jnp.mean(wide * wide, axis=-1, keepdims=True) + 1e-05) * gain


def pair_swap(values):
    n = lax.axis_size("req")
    return lax.ppermute(values, "req", [(i, i ^ 1) for i in range(n)])


def pair_join(core, mine, theirs, axis):
    first = jnp.concatenate([mine, theirs], axis=axis)
    second = jnp.concatenate([theirs, mine], axis=axis)
    return jnp.where(core == 0, first, second)


def ancestry(parents):
    size = parents.shape[-1]
    ids = jnp.arange(size, dtype=jnp.int32)
    reach = (parents[..., :, None] == ids).astype(jnp.float32) + jnp.eye(size, dtype=jnp.float32)
    for step in range(size.bit_length()):
        reach = jnp.minimum(
            jnp.einsum("...ij,...jk->...ik", reach, reach, precision=lax.Precision.HIGHEST), 1.0
        )
    return reach > 0.5


def attend(query, keys, values, live):
    scores = jnp.einsum("ikgd,tkd->ikgt", query, keys, preferred_element_type=jnp.float32) * HD ** (
        -0.5
    )
    mask = live[:, None, None, :]
    top = jnp.max(jnp.where(mask, scores, NEG), axis=-1)
    weights = jnp.where(mask, jnp.exp(scores - top[..., None]), 0.0).astype(jnp.bfloat16)
    total = jnp.sum(weights.astype(jnp.float32), axis=-1)
    acc = jnp.einsum("ikgt,tkd->ikgd", weights, values, preferred_element_type=jnp.float32)
    return (top, total, acc)


def finish(c_top, c_total, c_acc, d_top, d_total, d_acc):
    top = jnp.maximum(c_top, d_top)
    scale_c = jnp.exp(c_top - top)
    scale_d = jnp.exp(d_top - top)
    den = scale_c * c_total + scale_d * d_total
    num = c_acc * scale_c[..., None] + d_acc * scale_d[..., None]
    out = num / den[..., None]
    return out.reshape(out.shape[:-2] + (HEADS * HD,)).astype(jnp.bfloat16)


def on_device(
    tokens,
    parents,
    accepted,
    lengths,
    cache,
    attn_gain,
    qkv_weight,
    out_weight,
    moe_gain,
    router_weight,
    routes,
    gate_up_weight,
    down_weight,
):
    req_dev, draft, width = tokens.shape
    tok_rows = req_dev * draft
    group = HEADS // KVH
    q_width = HEADS * HD
    kv_width = KVH * HD
    span = cache.shape[1]
    group_req = cache.shape[0]
    n_req = lax.axis_size("req")
    kv_local = KVH // n_req
    q_local = HEADS // n_req
    flat = tokens.reshape(tok_rows, width)
    normed = rms_norm(flat, attn_gain).astype(jnp.bfloat16)
    core = lax.axis_index("req") % 2
    half = width // 2
    qkv_half = lax.dynamic_slice_in_dim(qkv_weight, core * half, half, axis=0)
    qkv_half = lax.all_gather(qkv_half, "exp", axis=1, tiled=True)
    out_rows = out_weight.shape[0] // 2
    out_half = lax.dynamic_slice_in_dim(out_weight, core * out_rows, out_rows, axis=0)
    qkv_half, out_half = lax.optimization_barrier((qkv_half, out_half))
    out_half = lax.all_gather(out_half, "exp", axis=0, tiled=True)
    both_rows = jnp.concatenate([normed, pair_swap(normed)], axis=0)
    both_half = lax.dynamic_slice_in_dim(both_rows, core * half, half, axis=1)
    qkv_part = jnp.dot(both_half, qkv_half, preferred_element_type=jnp.float32)
    qkv = (qkv_part[:tok_rows] + pair_swap(qkv_part[tok_rows:])).astype(jnp.bfloat16)
    queries = qkv[:, :q_width]
    draft_keys = qkv[:, q_width : q_width + kv_width]
    draft_values = qkv[:, q_width + kv_width :]
    send = jnp.concatenate(
        [
            queries.reshape(tok_rows, n_req, q_local * HD),
            draft_keys.reshape(tok_rows, n_req, kv_local * HD),
            draft_values.reshape(tok_rows, n_req, kv_local * HD),
        ],
        axis=-1,
    ).reshape(req_dev, draft, n_req, -1)
    piece = lax.all_to_all(send, "req", split_axis=2, concat_axis=0, tiled=True)
    count = piece.shape[1]
    q_all = piece[..., : q_local * HD].reshape(group_req, count, kv_local, group, HD)
    dk_all = piece[..., q_local * HD : (q_local + kv_local) * HD].reshape(
        group_req, count, kv_local, HD
    )
    dv_all = piece[..., (q_local + kv_local) * HD :].reshape(group_req, count, kv_local, HD)
    tree_all = ancestry(lax.all_gather(parents, "req", axis=0, tiled=True))
    d_top, d_total, d_acc = jax.vmap(attend)(q_all, dk_all, dv_all, tree_all)
    live_all = jnp.arange(span, dtype=jnp.int32)[None, :] < lengths[:, None]
    local_pairs = cache.reshape(group_req, span, kv_local, 2, HD)

    def cache_request(query_row, pair_row, live_row):
        return attend(query_row, pair_row[:, :, 0], pair_row[:, :, 1], live_row[None, :])

    c_top, c_total, c_acc = jax.vmap(cache_request)(q_all, local_pairs, live_all)
    top = jnp.maximum(c_top, d_top)
    scale_c = jnp.exp(c_top - top)
    scale_d = jnp.exp(d_top - top)
    den = scale_c * c_total + scale_d * d_total
    num = c_acc * scale_c[..., None] + d_acc * scale_d[..., None]
    head_out = (num / den[..., None]).astype(jnp.bfloat16)
    head_out = head_out.reshape(group_req, count, 1, q_local * HD)
    attn = lax.all_to_all(head_out, "req", split_axis=0, concat_axis=2, tiled=True)
    attn = attn.reshape(tok_rows, q_width)
    attn_rows = jnp.concatenate([attn, pair_swap(attn)], axis=0)
    n_shards = out_half.shape[0] // out_rows
    attn_half = lax.dynamic_index_in_dim(
        attn_rows.reshape(2 * tok_rows, n_shards, 2, out_rows), core, axis=2, keepdims=False
    ).reshape(2 * tok_rows, n_shards * out_rows)
    proj_part = jnp.dot(attn_half, out_half, preferred_element_type=jnp.float32)
    projected = proj_part[:tok_rows] + pair_swap(proj_part[tok_rows:])
    resid = flat.astype(jnp.float32) + projected
    moe_in = rms_norm(resid, moe_gain).astype(jnp.bfloat16)
    logits = jnp.dot(moe_in, router_weight, preferred_element_type=jnp.float32)
    experts = router_weight.shape[1]
    expert_ids = jnp.arange(experts, dtype=jnp.int32)
    chosen = routes.reshape(tok_rows, TOP)
    picked = jnp.sum(jnp.where(chosen[:, :, None] == expert_ids, logits[:, None, :], 0.0), axis=-1)
    gate_first = jax.nn.sigmoid(picked[:, 0] - picked[:, 1])
    gate_second = jax.nn.sigmoid(picked[:, 1] - picked[:, 0])
    capacity = max(2, 2 * tok_rows * TOP // experts)
    flat_ids = chosen.reshape(tok_rows * TOP)
    onehot = (flat_ids[:, None] == expert_ids).astype(jnp.int32)
    before = jnp.cumsum(onehot, axis=0) - onehot
    slot = jnp.sum(before * onehot, axis=1)
    position = (flat_ids * capacity + slot).reshape(tok_rows, TOP)
    select = position[:, :, None] == jnp.arange(experts * capacity, dtype=jnp.int32)
    placing = jnp.any(select, axis=1).astype(jnp.bfloat16)
    buffer = jnp.einsum("ts,td->sd", placing, moe_in, preferred_element_type=jnp.float32).astype(
        jnp.bfloat16
    )
    buffer = buffer.reshape(experts, capacity, width)
    received = lax.all_to_all(buffer, "exp", split_axis=0, concat_axis=0, tiled=True)
    count = received.shape[1]
    rows = received.reshape(experts * count, width)
    both = jnp.dot(rows, gate_up_weight[0], preferred_element_type=jnp.float32)
    hidden = (jax.nn.silu(both[:, :FF]) * both[:, FF:]).astype(jnp.bfloat16)
    result = jnp.dot(hidden, down_weight[0], preferred_element_type=jnp.float32).astype(
        jnp.bfloat16
    )
    back = lax.all_to_all(
        result.reshape(experts, count, width), "exp", split_axis=0, concat_axis=0, tiled=True
    )
    back_flat = back.reshape(experts * capacity, width)
    first = jnp.dot(
        select[:, 0].astype(jnp.bfloat16), back_flat, preferred_element_type=jnp.float32
    )
    second = jnp.dot(
        select[:, 1].astype(jnp.bfloat16), back_flat, preferred_element_type=jnp.float32
    )
    layer_out = (resid + gate_first[:, None] * first + gate_second[:, None] * second).astype(
        jnp.bfloat16
    )
    taking = (accepted[:, :, None] == jnp.arange(draft, dtype=jnp.int32)).astype(jnp.bfloat16)
    key_part = draft_keys.reshape(req_dev, draft, KVH, 1, HD)
    value_part = draft_values.reshape(req_dev, draft, KVH, 1, HD)
    kv_pairs = jnp.concatenate([key_part, value_part], axis=3).reshape(req_dev, draft, 2 * kv_width)
    appended = jnp.einsum(
        "rad,rdc->rac", taking, kv_pairs, preferred_element_type=jnp.float32
    ).astype(jnp.bfloat16)
    return (layer_out.reshape(req_dev, draft, width), appended)


def solution(mesh):
    placed = (
        P(("exp", "req"), None, None),
        P(("exp", "req"), None),
        P(("exp", "req"), None),
        P("exp"),
        P("exp", None, "req"),
        P(),
        P(None, "exp"),
        P("exp", None),
        P(),
        P(),
        P(("exp", "req"), None, None),
        P("exp", None, None),
        P("exp", None, None),
    )
    return jax.shard_map(
        on_device,
        mesh=mesh,
        in_specs=placed,
        out_specs=(P(("exp", "req"), None, None), P(("exp", "req"), None, None)),
        check_vma=False,
    )
```

```python
import jax
import jax.numpy as jnp
from jax import lax
from jax.sharding import PartitionSpec as P

HEADS = 24
KVH = 8
HD = 64
FF = 1024
TOP = 2


NEG = -1e30


def rms_norm(values, gain):
    wide = values.astype(jnp.float32)
    return wide * lax.rsqrt(jnp.mean(wide * wide, axis=-1, keepdims=True) + 1e-05) * gain


def pair_swap(values):
    n = lax.axis_size("req")
    return lax.ppermute(values, "req", [(i, i ^ 1) for i in range(n)])


def pair_join(core, mine, theirs, axis):
    first = jnp.concatenate([mine, theirs], axis=axis)
    second = jnp.concatenate([theirs, mine], axis=axis)
    return jnp.where(core == 0, first, second)


def ancestry(parents):
    size = parents.shape[-1]
    ids = jnp.arange(size, dtype=jnp.int32)
    reach = (parents[..., :, None] == ids).astype(jnp.float32) + jnp.eye(size, dtype=jnp.float32)
    for step in range(size.bit_length()):
        reach = jnp.minimum(
            jnp.einsum("...ij,...jk->...ik", reach, reach, precision=lax.Precision.HIGHEST), 1.0
        )
    return reach > 0.5


def attend(query, keys, values, live):
    scores = jnp.einsum("ikgd,tkd->ikgt", query, keys, preferred_element_type=jnp.float32) * HD ** (
        -0.5
    )
    mask = live[:, None, None, :]
    top = jnp.max(jnp.where(mask, scores, NEG), axis=-1)
    weights = jnp.where(mask, jnp.exp(scores - top[..., None]), 0.0).astype(jnp.bfloat16)
    total = jnp.sum(weights.astype(jnp.float32), axis=-1)
    acc = jnp.einsum("ikgt,tkd->ikgd", weights, values, preferred_element_type=jnp.float32)
    return (top, total, acc)


def finish(c_top, c_total, c_acc, d_top, d_total, d_acc):
    top = jnp.maximum(c_top, d_top)
    scale_c = jnp.exp(c_top - top)
    scale_d = jnp.exp(d_top - top)
    den = scale_c * c_total + scale_d * d_total
    num = c_acc * scale_c[..., None] + d_acc * scale_d[..., None]
    out = num / den[..., None]
    return out.reshape(out.shape[:-2] + (HEADS * HD,)).astype(jnp.bfloat16)


def on_device(
    tokens,
    parents,
    accepted,
    lengths,
    cache,
    attn_gain,
    qkv_weight,
    out_weight,
    moe_gain,
    router_weight,
    routes,
    gate_up_weight,
    down_weight,
):
    req_dev, draft, width = tokens.shape
    tok_rows = req_dev * draft
    group = HEADS // KVH
    q_width = HEADS * HD
    kv_width = KVH * HD
    span = cache.shape[1]
    group_req = cache.shape[0]
    n_req = lax.axis_size("req")
    kv_local = KVH // n_req
    q_local = HEADS // n_req
    flat = tokens.reshape(tok_rows, width)
    normed = rms_norm(flat, attn_gain).astype(jnp.bfloat16)
    core = lax.axis_index("req") % 2
    ring = 4
    quad = lax.axis_index("req") % ring
    base = lax.axis_index("req") - quad
    shard_cols = qkv_weight.shape[1]
    part_cols = shard_cols // ring
    qkv_part = lax.dynamic_slice_in_dim(qkv_weight, quad * part_cols, part_cols, axis=1)
    qkv_part = lax.all_gather(qkv_part, "exp", axis=1, tiled=True)
    half = width // 2
    out_rows = out_weight.shape[0] // 2
    out_half = lax.dynamic_slice_in_dim(out_weight, core * out_rows, out_rows, axis=0)
    qkv_part, out_half = lax.optimization_barrier((qkv_part, out_half))
    out_half = lax.all_gather(out_half, "exp", axis=0, tiled=True)
    n_shards = qkv_part.shape[1] // part_cols

    def quad_shift(values, step):
        pairs = [(i, i - i % ring + (i % ring + step) % ring) for i in range(n_req)]
        return lax.ppermute(values, "req", pairs)

    blocks = jnp.zeros((tok_rows, n_shards, ring, part_cols), jnp.bfloat16)
    for step in range(ring):
        rows_in = normed if step == 0 else quad_shift(normed, step)
        cols = jnp.dot(rows_in, qkv_part, preferred_element_type=jnp.float32).astype(
            jnp.bfloat16
        )
        if step != 0:
            cols = quad_shift(cols, ring - step)
        cols = cols.reshape(tok_rows, n_shards, 1, part_cols)
        blocks = lax.dynamic_update_slice_in_dim(blocks, cols, (quad + step) % ring, axis=2)
    qkv = blocks.reshape(tok_rows, n_shards * shard_cols)
    queries = qkv[:, :q_width]
    draft_keys = qkv[:, q_width : q_width + kv_width]
    draft_values = qkv[:, q_width + kv_width :]
    tree = ancestry(parents).reshape(tok_rows, 1, draft).astype(jnp.bfloat16)
    send = jnp.concatenate(
        [
            queries.reshape(tok_rows, n_req, q_local * HD),
            draft_keys.reshape(tok_rows, n_req, kv_local * HD),
            draft_values.reshape(tok_rows, n_req, kv_local * HD),
            jnp.broadcast_to(tree, (tok_rows, n_req, draft)),
        ],
        axis=-1,
    ).reshape(req_dev, draft, n_req, -1)
    piece = lax.all_to_all(send, "req", split_axis=2, concat_axis=0, tiled=True)
    count = piece.shape[1]
    q_all = piece[..., : q_local * HD].reshape(group_req, count, kv_local, group, HD)
    dk_all = piece[..., q_local * HD : (q_local + kv_local) * HD].reshape(
        group_req, count, kv_local, HD
    )
    kv_end = (q_local + 2 * kv_local) * HD
    dv_all = piece[..., (q_local + kv_local) * HD : kv_end].reshape(
        group_req, count, kv_local, HD
    )
    tree_all = piece[..., kv_end:].reshape(group_req, count, draft) > 0.5
    d_top, d_total, d_acc = jax.vmap(attend)(q_all, dk_all, dv_all, tree_all)
    live_all = jnp.arange(span, dtype=jnp.int32)[None, :] < lengths[:, None]
    local_pairs = cache.reshape(group_req, span, kv_local, 2, HD)

    def cache_request(query_row, pair_row, live_row):
        return attend(query_row, pair_row[:, :, 0], pair_row[:, :, 1], live_row[None, :])

    c_top, c_total, c_acc = jax.vmap(cache_request)(q_all, local_pairs, live_all)
    top = jnp.maximum(c_top, d_top)
    scale_c = jnp.exp(c_top - top)
    scale_d = jnp.exp(d_top - top)
    den = scale_c * c_total + scale_d * d_total
    num = c_acc * scale_c[..., None] + d_acc * scale_d[..., None]
    head_out = (num / den[..., None]).astype(jnp.bfloat16)
    head_out = head_out.reshape(group_req, count, 1, q_local * HD)
    attn = lax.all_to_all(head_out, "req", split_axis=0, concat_axis=2, tiled=True)
    attn = attn.reshape(tok_rows, q_width)
    attn_rows = jnp.concatenate([attn, pair_swap(attn)], axis=0)
    n_shards = out_half.shape[0] // out_rows
    attn_half = lax.dynamic_index_in_dim(
        attn_rows.reshape(2 * tok_rows, n_shards, 2, out_rows), core, axis=2, keepdims=False
    ).reshape(2 * tok_rows, n_shards * out_rows)
    proj_part = jnp.dot(attn_half, out_half, preferred_element_type=jnp.float32)
    projected = proj_part[:tok_rows] + pair_swap(proj_part[tok_rows:])
    resid = flat.astype(jnp.float32) + projected
    moe_in = rms_norm(resid, moe_gain).astype(jnp.bfloat16)
    logits = jnp.dot(moe_in, router_weight, preferred_element_type=jnp.float32)
    experts = router_weight.shape[1]
    expert_ids = jnp.arange(experts, dtype=jnp.int32)
    chosen = routes.reshape(tok_rows, TOP)
    picked = jnp.sum(jnp.where(chosen[:, :, None] == expert_ids, logits[:, None, :], 0.0), axis=-1)
    gate_first = jax.nn.sigmoid(picked[:, 0] - picked[:, 1])
    gate_second = jax.nn.sigmoid(picked[:, 1] - picked[:, 0])
    capacity = max(2, 2 * tok_rows * TOP // experts)
    flat_ids = chosen.reshape(tok_rows * TOP)
    onehot = (flat_ids[:, None] == expert_ids).astype(jnp.int32)
    before = jnp.cumsum(onehot, axis=0) - onehot
    slot = jnp.sum(before * onehot, axis=1)
    position = (flat_ids * capacity + slot).reshape(tok_rows, TOP)
    select = position[:, :, None] == jnp.arange(experts * capacity, dtype=jnp.int32)
    placing = jnp.any(select, axis=1).astype(jnp.bfloat16)
    buffer = jnp.einsum("ts,td->sd", placing, moe_in, preferred_element_type=jnp.float32).astype(
        jnp.bfloat16
    )
    buffer = buffer.reshape(experts, capacity, width)
    received = lax.all_to_all(buffer, "exp", split_axis=0, concat_axis=0, tiled=True)
    count = received.shape[1]
    rows = received.reshape(experts * count, width)
    both = jnp.dot(rows, gate_up_weight[0], preferred_element_type=jnp.float32)
    hidden = (jax.nn.silu(both[:, :FF]) * both[:, FF:]).astype(jnp.bfloat16)
    result = jnp.dot(hidden, down_weight[0], preferred_element_type=jnp.float32).astype(
        jnp.bfloat16
    )
    back = lax.all_to_all(
        result.reshape(experts, count, width), "exp", split_axis=0, concat_axis=0, tiled=True
    )
    back_flat = back.reshape(experts * capacity, width)
    first = jnp.dot(
        select[:, 0].astype(jnp.bfloat16), back_flat, preferred_element_type=jnp.float32
    )
    second = jnp.dot(
        select[:, 1].astype(jnp.bfloat16), back_flat, preferred_element_type=jnp.float32
    )
    layer_out = (resid + gate_first[:, None] * first + gate_second[:, None] * second).astype(
        jnp.bfloat16
    )
    taking = (accepted[:, :, None] == jnp.arange(draft, dtype=jnp.int32)).astype(jnp.bfloat16)
    key_part = draft_keys.reshape(req_dev, draft, KVH, 1, HD)
    value_part = draft_values.reshape(req_dev, draft, KVH, 1, HD)
    kv_pairs = jnp.concatenate([key_part, value_part], axis=3).reshape(req_dev, draft, 2 * kv_width)
    appended = jnp.einsum(
        "rad,rdc->rac", taking, kv_pairs, preferred_element_type=jnp.float32
    ).astype(jnp.bfloat16)
    return (layer_out.reshape(req_dev, draft, width), appended)


def solution(mesh):
    placed = (
        P(("exp", "req"), None, None),
        P(("exp", "req"), None),
        P(("exp", "req"), None),
        P("exp"),
        P("exp", None, "req"),
        P(),
        P(None, "exp"),
        P("exp", None),
        P(),
        P(),
        P(("exp", "req"), None, None),
        P("exp", None, None),
        P("exp", None, None),
    )
    return jax.shard_map(
        on_device,
        mesh=mesh,
        in_specs=placed,
        out_specs=(P(("exp", "req"), None, None), P(("exp", "req"), None, None)),
        check_vma=False,
    )
```

```python
import jax
import jax.numpy as jnp
from jax import lax
from jax.sharding import PartitionSpec as P

HEADS = 24
KVH = 8
HD = 64
FF = 1024
TOP = 2


NEG = -1e30


def rms_norm(values, gain):
    wide = values.astype(jnp.float32)
    return wide * lax.rsqrt(jnp.mean(wide * wide, axis=-1, keepdims=True) + 1e-05) * gain


def pair_swap(values):
    n = lax.axis_size("req")
    return lax.ppermute(values, "req", [(i, i ^ 1) for i in range(n)])


def pair_join(core, mine, theirs, axis):
    first = jnp.concatenate([mine, theirs], axis=axis)
    second = jnp.concatenate([theirs, mine], axis=axis)
    return jnp.where(core == 0, first, second)


def ancestry(parents):
    size = parents.shape[-1]
    ids = jnp.arange(size, dtype=jnp.int32)
    reach = (parents[..., :, None] == ids).astype(jnp.float32) + jnp.eye(size, dtype=jnp.float32)
    for step in range(size.bit_length()):
        reach = jnp.minimum(
            jnp.einsum("...ij,...jk->...ik", reach, reach, precision=lax.Precision.HIGHEST), 1.0
        )
    return reach > 0.5


def attend(query, keys, values, live):
    scores = jnp.einsum("ikgd,tkd->ikgt", query, keys, preferred_element_type=jnp.float32) * HD ** (
        -0.5
    )
    mask = live[:, None, None, :]
    top = jnp.max(jnp.where(mask, scores, NEG), axis=-1)
    weights = jnp.where(mask, jnp.exp(scores - top[..., None]), 0.0).astype(jnp.bfloat16)
    total = jnp.sum(weights.astype(jnp.float32), axis=-1)
    acc = jnp.einsum("ikgt,tkd->ikgd", weights, values, preferred_element_type=jnp.float32)
    return (top, total, acc)


def finish(c_top, c_total, c_acc, d_top, d_total, d_acc):
    top = jnp.maximum(c_top, d_top)
    scale_c = jnp.exp(c_top - top)
    scale_d = jnp.exp(d_top - top)
    den = scale_c * c_total + scale_d * d_total
    num = c_acc * scale_c[..., None] + d_acc * scale_d[..., None]
    out = num / den[..., None]
    return out.reshape(out.shape[:-2] + (HEADS * HD,)).astype(jnp.bfloat16)


def on_device(
    tokens,
    parents,
    accepted,
    lengths,
    cache,
    attn_gain,
    qkv_weight,
    out_weight,
    moe_gain,
    router_weight,
    routes,
    gate_up_weight,
    down_weight,
):
    req_dev, draft, width = tokens.shape
    tok_rows = req_dev * draft
    group = HEADS // KVH
    q_width = HEADS * HD
    kv_width = KVH * HD
    span = cache.shape[1]
    group_req = cache.shape[0]
    n_req = lax.axis_size("req")
    kv_local = KVH // n_req
    q_local = HEADS // n_req
    flat = tokens.reshape(tok_rows, width)
    normed = rms_norm(flat, attn_gain).astype(jnp.bfloat16)
    core = lax.axis_index("req") % 2
    ring = 4
    quad = lax.axis_index("req") % ring
    base = lax.axis_index("req") - quad
    shard_cols = qkv_weight.shape[1]
    part_cols = shard_cols // ring
    qkv_part = lax.dynamic_slice_in_dim(qkv_weight, quad * part_cols, part_cols, axis=1)
    n_shards = lax.axis_size("exp")
    qkv_part = lax.all_to_all(
        jnp.broadcast_to(qkv_part[None], (n_shards,) + qkv_part.shape),
        "exp",
        split_axis=0,
        concat_axis=0,
        tiled=True,
    )
    half = width // 2
    out_rows = out_weight.shape[0] // 2
    out_half = lax.dynamic_slice_in_dim(out_weight, core * out_rows, out_rows, axis=0)
    out_half = lax.all_gather(out_half, "exp", axis=0, tiled=True)

    def quad_shift(values, step):
        pairs = [(i, i - i % ring + (i % ring + step) % ring) for i in range(n_req)]
        return lax.ppermute(values, "req", pairs)

    rows_all = jnp.concatenate(
        [normed] + [quad_shift(normed, step) for step in range(1, ring)], axis=0
    )
    cols_all = jnp.einsum(
        "td,edj->tej", rows_all, qkv_part, preferred_element_type=jnp.float32
    ).astype(jnp.bfloat16)
    blocks = jnp.zeros((tok_rows, n_shards, ring, part_cols), jnp.bfloat16)
    for step in range(ring):
        cols = cols_all[step * tok_rows : (step + 1) * tok_rows]
        if step != 0:
            cols = quad_shift(cols, ring - step)
        cols = cols.reshape(tok_rows, n_shards, 1, part_cols)
        blocks = lax.dynamic_update_slice_in_dim(blocks, cols, (quad + step) % ring, axis=2)
    qkv = blocks.reshape(tok_rows, n_shards * shard_cols)
    queries = qkv[:, :q_width]
    draft_keys = qkv[:, q_width : q_width + kv_width]
    draft_values = qkv[:, q_width + kv_width :]
    tree = ancestry(parents).reshape(tok_rows, 1, draft).astype(jnp.bfloat16)
    send = jnp.concatenate(
        [
            queries.reshape(tok_rows, n_req, q_local * HD),
            draft_keys.reshape(tok_rows, n_req, kv_local * HD),
            draft_values.reshape(tok_rows, n_req, kv_local * HD),
            jnp.broadcast_to(tree, (tok_rows, n_req, draft)),
        ],
        axis=-1,
    ).reshape(req_dev, draft, n_req, -1)
    piece = lax.all_to_all(send, "req", split_axis=2, concat_axis=0, tiled=True)
    count = piece.shape[1]
    q_all = piece[..., : q_local * HD].reshape(group_req, count, kv_local, group, HD)
    dk_all = piece[..., q_local * HD : (q_local + kv_local) * HD].reshape(
        group_req, count, kv_local, HD
    )
    kv_end = (q_local + 2 * kv_local) * HD
    dv_all = piece[..., (q_local + kv_local) * HD : kv_end].reshape(
        group_req, count, kv_local, HD
    )
    tree_all = piece[..., kv_end:].reshape(group_req, count, draft) > 0.5
    d_top, d_total, d_acc = jax.vmap(attend)(q_all, dk_all, dv_all, tree_all)
    live_all = jnp.arange(span, dtype=jnp.int32)[None, :] < lengths[:, None]
    local_pairs = cache.reshape(group_req, span, kv_local, 2, HD)

    def cache_request(query_row, pair_row, live_row):
        return attend(query_row, pair_row[:, :, 0], pair_row[:, :, 1], live_row[None, :])

    c_top, c_total, c_acc = jax.vmap(cache_request)(q_all, local_pairs, live_all)
    top = jnp.maximum(c_top, d_top)
    scale_c = jnp.exp(c_top - top)
    scale_d = jnp.exp(d_top - top)
    den = scale_c * c_total + scale_d * d_total
    num = c_acc * scale_c[..., None] + d_acc * scale_d[..., None]
    head_out = (num / den[..., None]).astype(jnp.bfloat16)
    head_out = head_out.reshape(group_req, count, 1, q_local * HD)
    attn = lax.all_to_all(head_out, "req", split_axis=0, concat_axis=2, tiled=True)
    attn = attn.reshape(tok_rows, q_width)
    attn_rows = jnp.concatenate([attn, pair_swap(attn)], axis=0)
    n_shards = out_half.shape[0] // out_rows
    attn_half = lax.dynamic_index_in_dim(
        attn_rows.reshape(2 * tok_rows, n_shards, 2, out_rows), core, axis=2, keepdims=False
    ).reshape(2 * tok_rows, n_shards * out_rows)
    proj_part = jnp.dot(attn_half, out_half, preferred_element_type=jnp.float32)
    projected = proj_part[:tok_rows] + pair_swap(proj_part[tok_rows:])
    resid = flat.astype(jnp.float32) + projected
    moe_in = rms_norm(resid, moe_gain).astype(jnp.bfloat16)
    logits = jnp.dot(moe_in, router_weight, preferred_element_type=jnp.float32)
    experts = router_weight.shape[1]
    expert_ids = jnp.arange(experts, dtype=jnp.int32)
    chosen = routes.reshape(tok_rows, TOP)
    picked = jnp.sum(jnp.where(chosen[:, :, None] == expert_ids, logits[:, None, :], 0.0), axis=-1)
    gate_first = jax.nn.sigmoid(picked[:, 0] - picked[:, 1])
    gate_second = jax.nn.sigmoid(picked[:, 1] - picked[:, 0])
    capacity = max(2, 2 * tok_rows * TOP // experts)
    flat_ids = chosen.reshape(tok_rows * TOP)
    onehot = (flat_ids[:, None] == expert_ids).astype(jnp.int32)
    before = jnp.cumsum(onehot, axis=0) - onehot
    slot = jnp.sum(before * onehot, axis=1)
    position = (flat_ids * capacity + slot).reshape(tok_rows, TOP)
    select = position[:, :, None] == jnp.arange(experts * capacity, dtype=jnp.int32)
    placing = jnp.any(select, axis=1).astype(jnp.bfloat16)
    buffer = jnp.einsum("ts,td->sd", placing, moe_in, preferred_element_type=jnp.float32).astype(
        jnp.bfloat16
    )
    buffer = buffer.reshape(experts, capacity, width)
    received = lax.all_to_all(buffer, "exp", split_axis=0, concat_axis=0, tiled=True)
    count = received.shape[1]
    rows = received.reshape(experts * count, width)
    both = jnp.dot(rows, gate_up_weight[0], preferred_element_type=jnp.float32)
    hidden = (jax.nn.silu(both[:, :FF]) * both[:, FF:]).astype(jnp.bfloat16)
    result = jnp.dot(hidden, down_weight[0], preferred_element_type=jnp.float32).astype(
        jnp.bfloat16
    )
    back = lax.all_to_all(
        result.reshape(experts, count, width), "exp", split_axis=0, concat_axis=0, tiled=True
    )
    back_flat = back.reshape(experts * capacity, width)
    first = jnp.dot(
        select[:, 0].astype(jnp.bfloat16), back_flat, preferred_element_type=jnp.float32
    )
    second = jnp.dot(
        select[:, 1].astype(jnp.bfloat16), back_flat, preferred_element_type=jnp.float32
    )
    layer_out = (resid + gate_first[:, None] * first + gate_second[:, None] * second).astype(
        jnp.bfloat16
    )
    taking = (accepted[:, :, None] == jnp.arange(draft, dtype=jnp.int32)).astype(jnp.bfloat16)
    key_part = draft_keys.reshape(req_dev, draft, KVH, 1, HD)
    value_part = draft_values.reshape(req_dev, draft, KVH, 1, HD)
    kv_pairs = jnp.concatenate([key_part, value_part], axis=3).reshape(req_dev, draft, 2 * kv_width)
    appended = jnp.einsum(
        "rad,rdc->rac", taking, kv_pairs, preferred_element_type=jnp.float32
    ).astype(jnp.bfloat16)
    return (layer_out.reshape(req_dev, draft, width), appended)


def solution(mesh):
    placed = (
        P(("exp", "req"), None, None),
        P(("exp", "req"), None),
        P(("exp", "req"), None),
        P("exp"),
        P("exp", None, "req"),
        P(),
        P(None, "exp"),
        P("exp", None),
        P(),
        P(),
        P(("exp", "req"), None, None),
        P("exp", None, None),
        P("exp", None, None),
    )
    return jax.shard_map(
        on_device,
        mesh=mesh,
        in_specs=placed,
        out_specs=(P(("exp", "req"), None, None), P(("exp", "req"), None, None)),
        check_vma=False,
    )
```

```python
import jax
import jax.numpy as jnp
from jax import lax
from jax.sharding import PartitionSpec as P

HEADS = 24
KVH = 8
HD = 64
FF = 1024
TOP = 2


NEG = -1e30


def rms_norm(values, gain):
    wide = values.astype(jnp.float32)
    return wide * lax.rsqrt(jnp.mean(wide * wide, axis=-1, keepdims=True) + 1e-05) * gain


def pair_swap(values):
    n = lax.axis_size("req")
    return lax.ppermute(values, "req", [(i, i ^ 1) for i in range(n)])


def pair_join(core, mine, theirs, axis):
    first = jnp.concatenate([mine, theirs], axis=axis)
    second = jnp.concatenate([theirs, mine], axis=axis)
    return jnp.where(core == 0, first, second)


def ancestry(parents):
    size = parents.shape[-1]
    ids = jnp.arange(size, dtype=jnp.int32)
    reach = (parents[..., :, None] == ids).astype(jnp.float32) + jnp.eye(size, dtype=jnp.float32)
    for step in range(size.bit_length()):
        reach = jnp.minimum(
            jnp.einsum("...ij,...jk->...ik", reach, reach, precision=lax.Precision.HIGHEST), 1.0
        )
    return reach > 0.5


def attend(query, keys, values, live):
    scores = jnp.einsum("ikgd,tkd->ikgt", query, keys, preferred_element_type=jnp.float32) * HD ** (
        -0.5
    )
    mask = live[:, None, None, :]
    top = jnp.max(jnp.where(mask, scores, NEG), axis=-1)
    weights = jnp.where(mask, jnp.exp(scores - top[..., None]), 0.0).astype(jnp.bfloat16)
    total = jnp.sum(weights.astype(jnp.float32), axis=-1)
    acc = jnp.einsum("ikgt,tkd->ikgd", weights, values, preferred_element_type=jnp.float32)
    return (top, total, acc)


def finish(c_top, c_total, c_acc, d_top, d_total, d_acc):
    top = jnp.maximum(c_top, d_top)
    scale_c = jnp.exp(c_top - top)
    scale_d = jnp.exp(d_top - top)
    den = scale_c * c_total + scale_d * d_total
    num = c_acc * scale_c[..., None] + d_acc * scale_d[..., None]
    out = num / den[..., None]
    return out.reshape(out.shape[:-2] + (HEADS * HD,)).astype(jnp.bfloat16)


def on_device(
    tokens,
    parents,
    accepted,
    lengths,
    cache,
    attn_gain,
    qkv_weight,
    out_weight,
    moe_gain,
    router_weight,
    routes,
    gate_up_weight,
    down_weight,
):
    req_dev, draft, width = tokens.shape
    tok_rows = req_dev * draft
    group = HEADS // KVH
    q_width = HEADS * HD
    kv_width = KVH * HD
    span = cache.shape[1]
    group_req = cache.shape[0]
    n_req = lax.axis_size("req")
    kv_local = KVH // n_req
    q_local = HEADS // n_req
    flat = tokens.reshape(tok_rows, width)
    normed = rms_norm(flat, attn_gain).astype(jnp.bfloat16)
    core = lax.axis_index("req") % 2
    ring = 4
    quad = lax.axis_index("req") % ring
    base = lax.axis_index("req") - quad
    shard_cols = qkv_weight.shape[1]
    part_cols = shard_cols // ring
    qkv_part = lax.dynamic_slice_in_dim(qkv_weight, quad * part_cols, part_cols, axis=1)
    n_shards = lax.axis_size("exp")
    qkv_part = lax.all_to_all(
        jnp.broadcast_to(qkv_part[None], (n_shards,) + qkv_part.shape),
        "exp",
        split_axis=0,
        concat_axis=0,
        tiled=True,
    )
    half = width // 2
    out_rows = out_weight.shape[0] // 2
    out_half = lax.dynamic_slice_in_dim(out_weight, core * out_rows, out_rows, axis=0)
    qkv_part, out_half = lax.optimization_barrier((qkv_part, out_half))
    out_half = lax.all_gather(out_half, "exp", axis=0, tiled=True)

    def quad_shift(values, step):
        pairs = [(i, i - i % ring + (i % ring + step) % ring) for i in range(n_req)]
        return lax.ppermute(values, "req", pairs)

    rows_all = jnp.concatenate(
        [normed] + [quad_shift(normed, step) for step in range(1, ring)], axis=0
    )
    part_weight = jnp.transpose(qkv_part, (1, 0, 2)).reshape(width, n_shards * part_cols)
    cols_all = jnp.dot(rows_all, part_weight, preferred_element_type=jnp.float32).astype(
        jnp.bfloat16
    )
    blocks = jnp.zeros((ring, tok_rows, n_shards * part_cols), jnp.bfloat16)
    for step in range(ring):
        cols = cols_all[step * tok_rows : (step + 1) * tok_rows]
        if step != 0:
            cols = quad_shift(cols, ring - step)
        blocks = lax.dynamic_update_slice_in_dim(
            blocks, cols[None], (quad + step) % ring, axis=0
        )
    qkv = jnp.transpose(blocks.reshape(ring, tok_rows, n_shards, part_cols), (1, 2, 0, 3))
    qkv = qkv.reshape(tok_rows, n_shards * shard_cols)
    queries = qkv[:, :q_width]
    draft_keys = qkv[:, q_width : q_width + kv_width]
    draft_values = qkv[:, q_width + kv_width :]
    tree = ancestry(parents).reshape(tok_rows, 1, draft).astype(jnp.bfloat16)
    send = jnp.concatenate(
        [
            queries.reshape(tok_rows, n_req, q_local * HD),
            draft_keys.reshape(tok_rows, n_req, kv_local * HD),
            draft_values.reshape(tok_rows, n_req, kv_local * HD),
            jnp.broadcast_to(tree, (tok_rows, n_req, draft)),
        ],
        axis=-1,
    ).reshape(req_dev, draft, n_req, -1)
    piece = lax.all_to_all(send, "req", split_axis=2, concat_axis=0, tiled=True)
    count = piece.shape[1]
    q_all = piece[..., : q_local * HD].reshape(group_req, count, kv_local, group, HD)
    dk_all = piece[..., q_local * HD : (q_local + kv_local) * HD].reshape(
        group_req, count, kv_local, HD
    )
    kv_end = (q_local + 2 * kv_local) * HD
    dv_all = piece[..., (q_local + kv_local) * HD : kv_end].reshape(
        group_req, count, kv_local, HD
    )
    tree_all = piece[..., kv_end:].reshape(group_req, count, draft) > 0.5
    d_top, d_total, d_acc = jax.vmap(attend)(q_all, dk_all, dv_all, tree_all)
    live_all = jnp.arange(span, dtype=jnp.int32)[None, :] < lengths[:, None]
    local_pairs = cache.reshape(group_req, span, kv_local, 2, HD)

    def cache_request(query_row, pair_row, live_row):
        return attend(query_row, pair_row[:, :, 0], pair_row[:, :, 1], live_row[None, :])

    c_top, c_total, c_acc = jax.vmap(cache_request)(q_all, local_pairs, live_all)
    top = jnp.maximum(c_top, d_top)
    scale_c = jnp.exp(c_top - top)
    scale_d = jnp.exp(d_top - top)
    den = scale_c * c_total + scale_d * d_total
    num = c_acc * scale_c[..., None] + d_acc * scale_d[..., None]
    head_out = (num / den[..., None]).astype(jnp.bfloat16)
    head_out = head_out.reshape(group_req, count, 1, q_local * HD)
    attn = lax.all_to_all(head_out, "req", split_axis=0, concat_axis=2, tiled=True)
    attn = attn.reshape(tok_rows, q_width)
    attn_rows = jnp.concatenate([attn, pair_swap(attn)], axis=0)
    n_shards = out_half.shape[0] // out_rows
    attn_half = lax.dynamic_index_in_dim(
        attn_rows.reshape(2 * tok_rows, n_shards, 2, out_rows), core, axis=2, keepdims=False
    ).reshape(2 * tok_rows, n_shards * out_rows)
    proj_part = jnp.dot(attn_half, out_half, preferred_element_type=jnp.float32)
    projected = proj_part[:tok_rows] + pair_swap(proj_part[tok_rows:])
    resid = flat.astype(jnp.float32) + projected
    moe_in = rms_norm(resid, moe_gain).astype(jnp.bfloat16)
    logits = jnp.dot(moe_in, router_weight, preferred_element_type=jnp.float32)
    experts = router_weight.shape[1]
    expert_ids = jnp.arange(experts, dtype=jnp.int32)
    chosen = routes.reshape(tok_rows, TOP)
    picked = jnp.sum(jnp.where(chosen[:, :, None] == expert_ids, logits[:, None, :], 0.0), axis=-1)
    gate_first = jax.nn.sigmoid(picked[:, 0] - picked[:, 1])
    gate_second = jax.nn.sigmoid(picked[:, 1] - picked[:, 0])
    capacity = max(2, 2 * tok_rows * TOP // experts)
    flat_ids = chosen.reshape(tok_rows * TOP)
    onehot = (flat_ids[:, None] == expert_ids).astype(jnp.int32)
    before = jnp.cumsum(onehot, axis=0) - onehot
    slot = jnp.sum(before * onehot, axis=1)
    position = (flat_ids * capacity + slot).reshape(tok_rows, TOP)
    select = position[:, :, None] == jnp.arange(experts * capacity, dtype=jnp.int32)
    placing = jnp.any(select, axis=1).astype(jnp.bfloat16)
    buffer = jnp.einsum("ts,td->sd", placing, moe_in, preferred_element_type=jnp.float32).astype(
        jnp.bfloat16
    )
    buffer = buffer.reshape(experts, capacity, width)
    received = lax.all_to_all(buffer, "exp", split_axis=0, concat_axis=0, tiled=True)
    count = received.shape[1]
    rows = received.reshape(experts * count, width)
    both = jnp.dot(rows, gate_up_weight[0], preferred_element_type=jnp.float32)
    hidden = (jax.nn.silu(both[:, :FF]) * both[:, FF:]).astype(jnp.bfloat16)
    result = jnp.dot(hidden, down_weight[0], preferred_element_type=jnp.float32).astype(
        jnp.bfloat16
    )
    back = lax.all_to_all(
        result.reshape(experts, count, width), "exp", split_axis=0, concat_axis=0, tiled=True
    )
    back_flat = back.reshape(experts * capacity, width)
    first = jnp.dot(
        select[:, 0].astype(jnp.bfloat16), back_flat, preferred_element_type=jnp.float32
    )
    second = jnp.dot(
        select[:, 1].astype(jnp.bfloat16), back_flat, preferred_element_type=jnp.float32
    )
    layer_out = (resid + gate_first[:, None] * first + gate_second[:, None] * second).astype(
        jnp.bfloat16
    )
    taking = (accepted[:, :, None] == jnp.arange(draft, dtype=jnp.int32)).astype(jnp.bfloat16)
    key_part = draft_keys.reshape(req_dev, draft, KVH, 1, HD)
    value_part = draft_values.reshape(req_dev, draft, KVH, 1, HD)
    kv_pairs = jnp.concatenate([key_part, value_part], axis=3).reshape(req_dev, draft, 2 * kv_width)
    appended = jnp.einsum(
        "rad,rdc->rac", taking, kv_pairs, preferred_element_type=jnp.float32
    ).astype(jnp.bfloat16)
    return (layer_out.reshape(req_dev, draft, width), appended)


def solution(mesh):
    placed = (
        P(("exp", "req"), None, None),
        P(("exp", "req"), None),
        P(("exp", "req"), None),
        P("exp"),
        P("exp", None, "req"),
        P(),
        P(None, "exp"),
        P("exp", None),
        P(),
        P(),
        P(("exp", "req"), None, None),
        P("exp", None, None),
        P("exp", None, None),
    )
    return jax.shard_map(
        on_device,
        mesh=mesh,
        in_specs=placed,
        out_specs=(P(("exp", "req"), None, None), P(("exp", "req"), None, None)),
        check_vma=False,
    )
```

```python
import jax
import jax.numpy as jnp
from jax import lax
from jax.sharding import PartitionSpec as P

HEADS = 24
KVH = 8
HD = 64
FF = 1024
TOP = 2


NEG = -1e30


def rms_norm(values, gain):
    wide = values.astype(jnp.float32)
    return wide * lax.rsqrt(jnp.mean(wide * wide, axis=-1, keepdims=True) + 1e-05) * gain


def pair_swap(values):
    n = lax.axis_size("req")
    return lax.ppermute(values, "req", [(i, i ^ 1) for i in range(n)])


def pair_join(core, mine, theirs, axis):
    first = jnp.concatenate([mine, theirs], axis=axis)
    second = jnp.concatenate([theirs, mine], axis=axis)
    return jnp.where(core == 0, first, second)


def ancestry(parents):
    size = parents.shape[-1]
    ids = jnp.arange(size, dtype=jnp.int32)
    reach = (parents[..., :, None] == ids).astype(jnp.float32) + jnp.eye(size, dtype=jnp.float32)
    for step in range(size.bit_length()):
        reach = jnp.minimum(
            jnp.einsum("...ij,...jk->...ik", reach, reach, precision=lax.Precision.HIGHEST), 1.0
        )
    return reach > 0.5


def attend(query, keys, values, live):
    scores = jnp.einsum("ikgd,tkd->ikgt", query, keys, preferred_element_type=jnp.float32) * HD ** (
        -0.5
    )
    mask = live[:, None, None, :]
    top = jnp.max(jnp.where(mask, scores, NEG), axis=-1)
    weights = jnp.where(mask, jnp.exp(scores - top[..., None]), 0.0).astype(jnp.bfloat16)
    total = jnp.sum(weights.astype(jnp.float32), axis=-1)
    acc = jnp.einsum("ikgt,tkd->ikgd", weights, values, preferred_element_type=jnp.float32)
    return (top, total, acc)


def finish(c_top, c_total, c_acc, d_top, d_total, d_acc):
    top = jnp.maximum(c_top, d_top)
    scale_c = jnp.exp(c_top - top)
    scale_d = jnp.exp(d_top - top)
    den = scale_c * c_total + scale_d * d_total
    num = c_acc * scale_c[..., None] + d_acc * scale_d[..., None]
    out = num / den[..., None]
    return out.reshape(out.shape[:-2] + (HEADS * HD,)).astype(jnp.bfloat16)


def on_device(
    tokens,
    parents,
    accepted,
    lengths,
    cache,
    attn_gain,
    qkv_weight,
    out_weight,
    moe_gain,
    router_weight,
    routes,
    gate_up_weight,
    down_weight,
):
    req_dev, draft, width = tokens.shape
    tok_rows = req_dev * draft
    group = HEADS // KVH
    q_width = HEADS * HD
    kv_width = KVH * HD
    span = cache.shape[1]
    group_req = cache.shape[0]
    n_req = lax.axis_size("req")
    kv_local = KVH // n_req
    q_local = HEADS // n_req
    flat = tokens.reshape(tok_rows, width)
    normed = rms_norm(flat, attn_gain).astype(jnp.bfloat16)
    core = lax.axis_index("req") % 2
    ring = n_req
    quad = lax.axis_index("req") % ring
    base = lax.axis_index("req") - quad
    shard_cols = qkv_weight.shape[1]
    part_cols = shard_cols // ring
    qkv_part = lax.dynamic_slice_in_dim(qkv_weight, quad * part_cols, part_cols, axis=1)
    n_shards = lax.axis_size("exp")
    qkv_part = lax.all_to_all(
        jnp.broadcast_to(qkv_part[None], (n_shards,) + qkv_part.shape),
        "exp",
        split_axis=0,
        concat_axis=0,
        tiled=True,
    )
    half = width // 2
    out_rows = out_weight.shape[0] // 2
    out_half = lax.dynamic_slice_in_dim(out_weight, core * out_rows, out_rows, axis=0)
    out_half = lax.all_gather(out_half, "exp", axis=0, tiled=True)

    def quad_shift(values, step):
        pairs = [(i, i - i % ring + (i % ring + step) % ring) for i in range(n_req)]
        return lax.ppermute(values, "req", pairs)

    rows_all = jnp.concatenate(
        [normed] + [quad_shift(normed, step) for step in range(1, ring)], axis=0
    )
    part_weight = jnp.transpose(qkv_part, (1, 0, 2)).reshape(width, n_shards * part_cols)
    cols_all = jnp.dot(rows_all, part_weight, preferred_element_type=jnp.float32).astype(
        jnp.bfloat16
    )
    blocks = jnp.zeros((ring, tok_rows, n_shards * part_cols), jnp.bfloat16)
    for step in range(ring):
        cols = cols_all[step * tok_rows : (step + 1) * tok_rows]
        if step != 0:
            cols = quad_shift(cols, ring - step)
        blocks = lax.dynamic_update_slice_in_dim(
            blocks, cols[None], (quad + step) % ring, axis=0
        )
    qkv = jnp.transpose(blocks.reshape(ring, tok_rows, n_shards, part_cols), (1, 2, 0, 3))
    qkv = qkv.reshape(tok_rows, n_shards * shard_cols)
    queries = qkv[:, :q_width]
    draft_keys = qkv[:, q_width : q_width + kv_width]
    draft_values = qkv[:, q_width + kv_width :]
    tree = ancestry(parents).reshape(tok_rows, 1, draft).astype(jnp.bfloat16)
    send = jnp.concatenate(
        [
            queries.reshape(tok_rows, n_req, q_local * HD),
            draft_keys.reshape(tok_rows, n_req, kv_local * HD),
            draft_values.reshape(tok_rows, n_req, kv_local * HD),
            jnp.broadcast_to(tree, (tok_rows, n_req, draft)),
        ],
        axis=-1,
    ).reshape(req_dev, draft, n_req, -1)
    piece = lax.all_to_all(send, "req", split_axis=2, concat_axis=0, tiled=True)
    count = piece.shape[1]
    q_all = piece[..., : q_local * HD].reshape(group_req, count, kv_local, group, HD)
    dk_all = piece[..., q_local * HD : (q_local + kv_local) * HD].reshape(
        group_req, count, kv_local, HD
    )
    kv_end = (q_local + 2 * kv_local) * HD
    dv_all = piece[..., (q_local + kv_local) * HD : kv_end].reshape(
        group_req, count, kv_local, HD
    )
    tree_all = piece[..., kv_end:].reshape(group_req, count, draft) > 0.5
    d_top, d_total, d_acc = jax.vmap(attend)(q_all, dk_all, dv_all, tree_all)
    live_all = jnp.arange(span, dtype=jnp.int32)[None, :] < lengths[:, None]
    local_pairs = cache.reshape(group_req, span, kv_local, 2, HD)

    def cache_request(query_row, pair_row, live_row):
        return attend(query_row, pair_row[:, :, 0], pair_row[:, :, 1], live_row[None, :])

    c_top, c_total, c_acc = jax.vmap(cache_request)(q_all, local_pairs, live_all)
    top = jnp.maximum(c_top, d_top)
    scale_c = jnp.exp(c_top - top)
    scale_d = jnp.exp(d_top - top)
    den = scale_c * c_total + scale_d * d_total
    num = c_acc * scale_c[..., None] + d_acc * scale_d[..., None]
    head_out = (num / den[..., None]).astype(jnp.bfloat16)
    head_out = head_out.reshape(group_req, count, 1, q_local * HD)
    attn = lax.all_to_all(head_out, "req", split_axis=0, concat_axis=2, tiled=True)
    attn = attn.reshape(tok_rows, q_width)
    attn_rows = jnp.concatenate([attn, pair_swap(attn)], axis=0)
    n_shards = out_half.shape[0] // out_rows
    attn_half = lax.dynamic_index_in_dim(
        attn_rows.reshape(2 * tok_rows, n_shards, 2, out_rows), core, axis=2, keepdims=False
    ).reshape(2 * tok_rows, n_shards * out_rows)
    proj_part = jnp.dot(attn_half, out_half, preferred_element_type=jnp.float32)
    projected = proj_part[:tok_rows] + pair_swap(proj_part[tok_rows:])
    resid = flat.astype(jnp.float32) + projected
    moe_in = rms_norm(resid, moe_gain).astype(jnp.bfloat16)
    logits = jnp.dot(moe_in, router_weight, preferred_element_type=jnp.float32)
    experts = router_weight.shape[1]
    expert_ids = jnp.arange(experts, dtype=jnp.int32)
    chosen = routes.reshape(tok_rows, TOP)
    picked = jnp.sum(jnp.where(chosen[:, :, None] == expert_ids, logits[:, None, :], 0.0), axis=-1)
    gate_first = jax.nn.sigmoid(picked[:, 0] - picked[:, 1])
    gate_second = jax.nn.sigmoid(picked[:, 1] - picked[:, 0])
    capacity = max(2, 2 * tok_rows * TOP // experts)
    flat_ids = chosen.reshape(tok_rows * TOP)
    onehot = (flat_ids[:, None] == expert_ids).astype(jnp.int32)
    before = jnp.cumsum(onehot, axis=0) - onehot
    slot = jnp.sum(before * onehot, axis=1)
    position = (flat_ids * capacity + slot).reshape(tok_rows, TOP)
    select = position[:, :, None] == jnp.arange(experts * capacity, dtype=jnp.int32)
    placing = jnp.any(select, axis=1).astype(jnp.bfloat16)
    buffer = jnp.einsum("ts,td->sd", placing, moe_in, preferred_element_type=jnp.float32).astype(
        jnp.bfloat16
    )
    buffer = buffer.reshape(experts, capacity, width)
    received = lax.all_to_all(buffer, "exp", split_axis=0, concat_axis=0, tiled=True)
    count = received.shape[1]
    rows = received.reshape(experts * count, width)
    both = jnp.dot(rows, gate_up_weight[0], preferred_element_type=jnp.float32)
    hidden = (jax.nn.silu(both[:, :FF]) * both[:, FF:]).astype(jnp.bfloat16)
    result = jnp.dot(hidden, down_weight[0], preferred_element_type=jnp.float32).astype(
        jnp.bfloat16
    )
    back = lax.all_to_all(
        result.reshape(experts, count, width), "exp", split_axis=0, concat_axis=0, tiled=True
    )
    back_flat = back.reshape(experts * capacity, width)
    first = jnp.dot(
        select[:, 0].astype(jnp.bfloat16), back_flat, preferred_element_type=jnp.float32
    )
    second = jnp.dot(
        select[:, 1].astype(jnp.bfloat16), back_flat, preferred_element_type=jnp.float32
    )
    layer_out = (resid + gate_first[:, None] * first + gate_second[:, None] * second).astype(
        jnp.bfloat16
    )
    taking = (accepted[:, :, None] == jnp.arange(draft, dtype=jnp.int32)).astype(jnp.bfloat16)
    key_part = draft_keys.reshape(req_dev, draft, KVH, 1, HD)
    value_part = draft_values.reshape(req_dev, draft, KVH, 1, HD)
    kv_pairs = jnp.concatenate([key_part, value_part], axis=3).reshape(req_dev, draft, 2 * kv_width)
    appended = jnp.einsum(
        "rad,rdc->rac", taking, kv_pairs, preferred_element_type=jnp.float32
    ).astype(jnp.bfloat16)
    return (layer_out.reshape(req_dev, draft, width), appended)


def solution(mesh):
    placed = (
        P(("exp", "req"), None, None),
        P(("exp", "req"), None),
        P(("exp", "req"), None),
        P("exp"),
        P("exp", None, "req"),
        P(),
        P(None, "exp"),
        P("exp", None),
        P(),
        P(),
        P(("exp", "req"), None, None),
        P("exp", None, None),
        P("exp", None, None),
    )
    return jax.shard_map(
        on_device,
        mesh=mesh,
        in_specs=placed,
        out_specs=(P(("exp", "req"), None, None), P(("exp", "req"), None, None)),
        check_vma=False,
    )
```

```python
import jax
import jax.numpy as jnp
from jax import lax
from jax.sharding import PartitionSpec as P

HEADS = 24
KVH = 8
HD = 64
FF = 1024
TOP = 2


NEG = -1e30


def rms_norm(values, gain):
    wide = values.astype(jnp.float32)
    return wide * lax.rsqrt(jnp.mean(wide * wide, axis=-1, keepdims=True) + 1e-05) * gain


def pair_swap(values):
    n = lax.axis_size("req")
    return lax.ppermute(values, "req", [(i, i ^ 1) for i in range(n)])


def pair_join(core, mine, theirs, axis):
    first = jnp.concatenate([mine, theirs], axis=axis)
    second = jnp.concatenate([theirs, mine], axis=axis)
    return jnp.where(core == 0, first, second)


def ancestry(parents):
    size = parents.shape[-1]
    ids = jnp.arange(size, dtype=jnp.int32)
    reach = (parents[..., :, None] == ids).astype(jnp.float32) + jnp.eye(size, dtype=jnp.float32)
    for step in range(size.bit_length()):
        reach = jnp.minimum(
            jnp.einsum("...ij,...jk->...ik", reach, reach, precision=lax.Precision.HIGHEST), 1.0
        )
    return reach > 0.5


def attend(query, keys, values, live):
    scores = jnp.einsum("ikgd,tkd->ikgt", query, keys, preferred_element_type=jnp.float32) * HD ** (
        -0.5
    )
    mask = live[:, None, None, :]
    top = jnp.max(jnp.where(mask, scores, NEG), axis=-1)
    weights = jnp.where(mask, jnp.exp(scores - top[..., None]), 0.0).astype(jnp.bfloat16)
    total = jnp.sum(weights.astype(jnp.float32), axis=-1)
    acc = jnp.einsum("ikgt,tkd->ikgd", weights, values, preferred_element_type=jnp.float32)
    return (top, total, acc)


def finish(c_top, c_total, c_acc, d_top, d_total, d_acc):
    top = jnp.maximum(c_top, d_top)
    scale_c = jnp.exp(c_top - top)
    scale_d = jnp.exp(d_top - top)
    den = scale_c * c_total + scale_d * d_total
    num = c_acc * scale_c[..., None] + d_acc * scale_d[..., None]
    out = num / den[..., None]
    return out.reshape(out.shape[:-2] + (HEADS * HD,)).astype(jnp.bfloat16)


def on_device(
    tokens,
    parents,
    accepted,
    lengths,
    cache,
    attn_gain,
    qkv_weight,
    out_weight,
    moe_gain,
    router_weight,
    routes,
    gate_up_weight,
    down_weight,
):
    req_dev, draft, width = tokens.shape
    tok_rows = req_dev * draft
    group = HEADS // KVH
    q_width = HEADS * HD
    kv_width = KVH * HD
    span = cache.shape[1]
    group_req = cache.shape[0]
    n_req = lax.axis_size("req")
    kv_local = KVH // n_req
    q_local = HEADS // n_req
    flat = tokens.reshape(tok_rows, width)
    normed = rms_norm(flat, attn_gain).astype(jnp.bfloat16)
    core = lax.axis_index("req") % 2
    ring = n_req
    quad = lax.axis_index("req") % ring
    base = lax.axis_index("req") - quad
    shard_cols = qkv_weight.shape[1]
    part_cols = shard_cols // ring
    qkv_part = lax.dynamic_slice_in_dim(qkv_weight, quad * part_cols, part_cols, axis=1)
    n_shards = lax.axis_size("exp")
    qkv_part = lax.all_to_all(
        jnp.broadcast_to(qkv_part[None], (n_shards,) + qkv_part.shape),
        "exp",
        split_axis=0,
        concat_axis=0,
        tiled=True,
    )
    half = width // 2
    out_rows = out_weight.shape[0] // 2
    out_half = lax.dynamic_slice_in_dim(out_weight, core * out_rows, out_rows, axis=0)
    out_half = lax.all_gather(out_half, "exp", axis=0, tiled=True)

    def quad_shift(values, step):
        pairs = [(i, i - i % ring + (i % ring + step) % ring) for i in range(n_req)]
        return lax.ppermute(values, "req", pairs)

    rows_all = jnp.concatenate(
        [normed] + [quad_shift(normed, step) for step in range(1, ring)], axis=0
    )
    part_weight = jnp.transpose(qkv_part, (1, 0, 2)).reshape(width, n_shards * part_cols)
    cols_all = jnp.dot(rows_all, part_weight, preferred_element_type=jnp.float32).astype(
        jnp.bfloat16
    )
    blocks = []
    for step in range(ring):
        cols = cols_all[step * tok_rows : (step + 1) * tok_rows]
        if step != 0:
            cols = quad_shift(cols, ring - step)
        blocks.append(cols)
    blocks = jnp.roll(jnp.stack(blocks), quad, axis=0)
    qkv = jnp.transpose(blocks.reshape(ring, tok_rows, n_shards, part_cols), (1, 2, 0, 3))
    qkv = qkv.reshape(tok_rows, n_shards * shard_cols)
    queries = qkv[:, :q_width]
    draft_keys = qkv[:, q_width : q_width + kv_width]
    draft_values = qkv[:, q_width + kv_width :]
    tree = ancestry(parents).reshape(tok_rows, 1, draft).astype(jnp.bfloat16)
    send = jnp.concatenate(
        [
            queries.reshape(tok_rows, n_req, q_local * HD),
            draft_keys.reshape(tok_rows, n_req, kv_local * HD),
            draft_values.reshape(tok_rows, n_req, kv_local * HD),
            jnp.broadcast_to(tree, (tok_rows, n_req, draft)),
        ],
        axis=-1,
    ).reshape(req_dev, draft, n_req, -1)
    piece = lax.all_to_all(send, "req", split_axis=2, concat_axis=0, tiled=True)
    count = piece.shape[1]
    q_all = piece[..., : q_local * HD].reshape(group_req, count, kv_local, group, HD)
    dk_all = piece[..., q_local * HD : (q_local + kv_local) * HD].reshape(
        group_req, count, kv_local, HD
    )
    kv_end = (q_local + 2 * kv_local) * HD
    dv_all = piece[..., (q_local + kv_local) * HD : kv_end].reshape(
        group_req, count, kv_local, HD
    )
    tree_all = piece[..., kv_end:].reshape(group_req, count, draft) > 0.5
    d_top, d_total, d_acc = jax.vmap(attend)(q_all, dk_all, dv_all, tree_all)
    live_all = jnp.arange(span, dtype=jnp.int32)[None, :] < lengths[:, None]
    local_pairs = cache.reshape(group_req, span, kv_local, 2, HD)

    def cache_request(query_row, pair_row, live_row):
        return attend(query_row, pair_row[:, :, 0], pair_row[:, :, 1], live_row[None, :])

    c_top, c_total, c_acc = jax.vmap(cache_request)(q_all, local_pairs, live_all)
    top = jnp.maximum(c_top, d_top)
    scale_c = jnp.exp(c_top - top)
    scale_d = jnp.exp(d_top - top)
    den = scale_c * c_total + scale_d * d_total
    num = c_acc * scale_c[..., None] + d_acc * scale_d[..., None]
    head_out = (num / den[..., None]).astype(jnp.bfloat16)
    head_out = head_out.reshape(group_req, count, 1, q_local * HD)
    attn = lax.all_to_all(head_out, "req", split_axis=0, concat_axis=2, tiled=True)
    attn = attn.reshape(tok_rows, q_width)
    attn_rows = jnp.concatenate([attn, pair_swap(attn)], axis=0)
    n_shards = out_half.shape[0] // out_rows
    attn_half = lax.dynamic_index_in_dim(
        attn_rows.reshape(2 * tok_rows, n_shards, 2, out_rows), core, axis=2, keepdims=False
    ).reshape(2 * tok_rows, n_shards * out_rows)
    proj_part = jnp.dot(attn_half, out_half, preferred_element_type=jnp.float32)
    projected = proj_part[:tok_rows] + pair_swap(proj_part[tok_rows:])
    resid = flat.astype(jnp.float32) + projected
    moe_in = rms_norm(resid, moe_gain).astype(jnp.bfloat16)
    logits = jnp.dot(moe_in, router_weight, preferred_element_type=jnp.float32)
    experts = router_weight.shape[1]
    expert_ids = jnp.arange(experts, dtype=jnp.int32)
    chosen = routes.reshape(tok_rows, TOP)
    picked = jnp.sum(jnp.where(chosen[:, :, None] == expert_ids, logits[:, None, :], 0.0), axis=-1)
    gate_first = jax.nn.sigmoid(picked[:, 0] - picked[:, 1])
    gate_second = jax.nn.sigmoid(picked[:, 1] - picked[:, 0])
    capacity = max(2, 2 * tok_rows * TOP // experts)
    flat_ids = chosen.reshape(tok_rows * TOP)
    onehot = (flat_ids[:, None] == expert_ids).astype(jnp.int32)
    before = jnp.cumsum(onehot, axis=0) - onehot
    slot = jnp.sum(before * onehot, axis=1)
    position = (flat_ids * capacity + slot).reshape(tok_rows, TOP)
    select = position[:, :, None] == jnp.arange(experts * capacity, dtype=jnp.int32)
    placing = jnp.any(select, axis=1).astype(jnp.bfloat16)
    buffer = jnp.einsum("ts,td->sd", placing, moe_in, preferred_element_type=jnp.float32).astype(
        jnp.bfloat16
    )
    buffer = buffer.reshape(experts, capacity, width)
    received = lax.all_to_all(buffer, "exp", split_axis=0, concat_axis=0, tiled=True)
    count = received.shape[1]
    rows = received.reshape(experts * count, width)
    both = jnp.dot(rows, gate_up_weight[0], preferred_element_type=jnp.float32)
    hidden = (jax.nn.silu(both[:, :FF]) * both[:, FF:]).astype(jnp.bfloat16)
    result = jnp.dot(hidden, down_weight[0], preferred_element_type=jnp.float32).astype(
        jnp.bfloat16
    )
    back = lax.all_to_all(
        result.reshape(experts, count, width), "exp", split_axis=0, concat_axis=0, tiled=True
    )
    back_flat = back.reshape(experts * capacity, width)
    first = jnp.dot(
        select[:, 0].astype(jnp.bfloat16), back_flat, preferred_element_type=jnp.float32
    )
    second = jnp.dot(
        select[:, 1].astype(jnp.bfloat16), back_flat, preferred_element_type=jnp.float32
    )
    layer_out = (resid + gate_first[:, None] * first + gate_second[:, None] * second).astype(
        jnp.bfloat16
    )
    taking = (accepted[:, :, None] == jnp.arange(draft, dtype=jnp.int32)).astype(jnp.bfloat16)
    key_part = draft_keys.reshape(req_dev, draft, KVH, 1, HD)
    value_part = draft_values.reshape(req_dev, draft, KVH, 1, HD)
    kv_pairs = jnp.concatenate([key_part, value_part], axis=3).reshape(req_dev, draft, 2 * kv_width)
    appended = jnp.einsum(
        "rad,rdc->rac", taking, kv_pairs, preferred_element_type=jnp.float32
    ).astype(jnp.bfloat16)
    return (layer_out.reshape(req_dev, draft, width), appended)


def solution(mesh):
    placed = (
        P(("exp", "req"), None, None),
        P(("exp", "req"), None),
        P(("exp", "req"), None),
        P("exp"),
        P("exp", None, "req"),
        P(),
        P(None, "exp"),
        P("exp", None),
        P(),
        P(),
        P(("exp", "req"), None, None),
        P("exp", None, None),
        P("exp", None, None),
    )
    return jax.shard_map(
        on_device,
        mesh=mesh,
        in_specs=placed,
        out_specs=(P(("exp", "req"), None, None), P(("exp", "req"), None, None)),
        check_vma=False,
    )
```
